256 devices in a mesh: fsdp: 32 (over z, x_hi, core), tensor: 8 (over x_lo, y).
Axes of the slice: x: 4 (x_hi: 2, x_lo: 2; x = x_hi * 2 + x_lo), y: 4, z: 8, core: 2. Of those that a mesh axis runs over, the one named last changes fastest.
Arguments:
- tokens: bfloat16 [49152, 8192], P(('fsdp', 'tensor'))
- gain: bfloat16 [8192], replicated, may hold values from 0.5 to 1.5
- kv_weight: bfloat16 [8192, 2048], P('fsdp', 'tensor'), may hold values from -0.09375 to 0.09375
- block_mask: int32 [64, 16], P('fsdp', 'tensor'), may hold values from 0 to 1
- cotangent: bfloat16 [49152, 2048], P('fsdp', 'tensor'), may hold values from -0.02734375 to 0.02734375
Outputs:
- projected: bfloat16 [49152, 2048], P('fsdp', 'tensor')
- weight_grad: float32 [8192, 2048], P('fsdp', 'tensor')
The draws below stay inside these ranges and needn't reach their ends.
All inputs are finite; a program needn't handle non-finite values.
Results may differ from the reference program's by a relative error of at most 0.005.
Values may be sent and summed in bfloat16 or wider, within the bound.
A program may use at most 128 MiB of HBM per device.

```python
import math
import jax
import jax.numpy as jnp
from jax import lax

D = 8192
KVW = 2048
BLOCK = 128
TOKENS = 49152


def draw_tokens(key, part):
    first, second = jax.random.split(key, 2)
    scale = jnp.exp(jax.random.uniform(second, (TOKENS, 1), jnp.float32) * math.log(10.0))
    values = jax.random.normal(first, (TOKENS, D), jnp.float32) * scale
    return values.astype(jnp.bfloat16)


def draw_block_mask(key, part):
    first, second = jax.random.split(jax.random.fold_in(key, 17))
    density = jax.random.randint(first, (D // BLOCK, 1), 20, 81)
    trial = jax.random.randint(second, (D // BLOCK, KVW // BLOCK), 0, 100)
    return jnp.where(trial < density, 1, 0).astype(jnp.int32)


def shard_levels(own_key, shape, cuts, least, top_value):
    level, own = 1.0, jax.random.fold_in(own_key, 6)
    for position, shards_of in cuts:
        draws = jnp.exp(jax.random.uniform(jax.random.fold_in(own, position), (shards_of,), jnp.float32, least / len(cuts), top_value / len(cuts)))
        level = level * jnp.repeat(draws, shape[position] // shards_of).reshape([-1 if axis == position else 1 for axis in range(len(shape))])
    return level


def gaussian(rng, dims, scale, reach, cuts=(), dtype=jnp.bfloat16):
    values = jax.random.normal(rng, dims, jnp.float32) * scale
    if len(cuts) > 0:
        values = shard_levels(rng, dims, cuts, -0.22, 0.18) * values
    return jnp.clip(values, min=-reach, max=reach).astype(dtype)


def setup_inputs(seed: int = 0) -> dict:
    keys = jax.random.split(jax.random.key(seed), 6)
    tokens = draw_tokens(jax.random.fold_in(keys[5], 71), 0)
    gain = jnp.clip(1.0 + 0.1 * jax.random.normal(keys[1], (D,), jnp.float32), 0.5, 1.5).astype(jnp.bfloat16)
    kv_weight = gaussian(keys[2], (D, KVW), (D // 2) ** -0.5, 0.09375, ((0, 32), (1, 8)))
    block_mask = draw_block_mask(jax.random.fold_in(keys[5], 71), 0)
    cotangent = gaussian(keys[4], (TOKENS, KVW), TOKENS ** -0.5, 0.02734375, ((0, 32), (1, 8)))
    return {"tokens": tokens, "gain": gain, "kv_weight": kv_weight, "block_mask": block_mask, "cotangent": cotangent}


def expand_mask(block_mask):
    wide = jnp.repeat(block_mask, BLOCK, axis=0)
    return jnp.repeat(wide, BLOCK, axis=1).astype(jnp.float32)

def reference(tokens, gain, kv_weight, block_mask, cotangent):
    values = tokens.astype(jnp.float32)
    square = lax.optimization_barrier(jnp.mean(values * values, axis=-1, keepdims=True))
    normed = (values * lax.rsqrt(square + 1e-05) * gain.astype(jnp.float32)).astype(jnp.bfloat16)
    full_mask = expand_mask(block_mask)
    masked = (kv_weight.astype(jnp.float32) * full_mask).astype(jnp.bfloat16)
    projected = jnp.dot(normed, masked, preferred_element_type=jnp.float32).astype(jnp.bfloat16)
    product = lax.dot_general(normed, cotangent, (((0,), (0,)), ((), ())), preferred_element_type=jnp.float32)
    weight_grad = product * full_mask
    return (projected, weight_grad)
```

```python
import jax
import jax.numpy as jnp
from jax import lax
from jax.experimental import pallas as pl
from jax.experimental.pallas import tpu as pltpu
from jax.sharding import PartitionSpec as P

MESH = pl.DeviceIdType.MESH
NZ, NX, NC, NY = 8, 4, 2, 4
BLOCK = 128


def kernel(
    tokens, gain, weight, mask, cot, proj, grad,
    normed, scale, masked, cot_in, cot_t, part, core_in, keep, x_out, x_in,
    z_out, z_in, acc, p_out, p_in,
    y_send, y_recv, w_send, w_recv, wz_send, wz_recv, wd_send, wd_recv,
    c_send, c_recv, x_send, x_recv, z_send, z_recv, o_send, o_recv,
):
    rows = tokens.shape[0]
    group = NY * rows
    side = weight.shape[0]
    wide = 4 * side
    f, t = lax.axis_index("fsdp"), lax.axis_index("tensor")
    z, xh, c = lax.div(f, 4), lax.rem(lax.div(f, 2), 2), lax.rem(f, 2)
    xl, y = lax.div(t, NY), lax.rem(t, NY)
    x = xh * 2 + xl
    q = x * 2 + c
    yp, ym, y2 = lax.rem(y + 1, NY), lax.rem(y + 3, NY), lax.rem(y + 2, NY)
    zp, zm = lax.rem(z + 1, NZ), lax.rem(z + NZ - 1, NZ)

    def dev(zz, xx, cc, yy):
        return ((zz * 2 + lax.div(xx, 2)) * 2 + cc, lax.rem(xx, 2) * NY + yy)

    def chunk(k):
        return lax.rem(z + 1 + k, NZ)

    def copy(src, dst, send, recv, to):
        return pltpu.make_async_remote_copy(
            src_ref=src, dst_ref=dst, send_sem=send, recv_sem=recv, device_id=to, device_id_type=MESH
        )

    sibling = dev(z, x, 1 - c, y)
    beside = dev(z, xh * 2 + 1 - xl, c, y)
    up, down = dev(z, x, c, yp), dev(z, x, c, ym)

    barrier = pltpu.get_barrier_semaphore()

    def greet(to):
        pl.semaphore_signal(barrier, inc=1, device_id=to, device_id_type=MESH)

    greet(up)
    greet(down)
    for r in range(1, 8):
        p = lax.rem(q + r, 8)
        greet(dev(z, lax.div(p, 2), lax.rem(p, 2), y))
        greet(dev(lax.rem(z + r, NZ), x, c, y))

    own_j = xh * 2 + c
    for a in range(side // BLOCK):
        for b in range(side // BLOCK):
            at = (pl.ds(a * BLOCK, BLOCK), pl.ds(b * BLOCK, BLOCK))
            m = mask[a, b].astype(jnp.float32)
            masked[z, own_j, xl, at[0], at[1]] = (weight[at].astype(jnp.float32) * m).astype(jnp.bfloat16)

    @pl.loop(0, rows // 16)
    def _(r):
        at = pl.ds(pl.multiple_of(r * 16, 16), 16)
        v = tokens[at, :].astype(jnp.float32)
        square = jnp.mean(v * v, axis=-1, keepdims=True)
        scale[at, :] = jnp.broadcast_to(lax.rsqrt(square + 1e-05), (16, side))

    def normalize(k):
        zc = chunk(k)

        @pl.loop(0, 4)
        def _(j):
            at = pl.ds(pl.multiple_of(zc * wide + j * side, side), side)
            v = tokens[:, at].astype(jnp.float32)
            g = gain[:, at].astype(jnp.float32)
            normed[zc, y, j] = (v * scale[...] * g).astype(jnp.bfloat16)

    def direct(k, way):
        zc = chunk(k)
        return copy(
            normed.at[zc, y], normed.at[zc, y], y_send.at[k, way], y_recv.at[k, way], down if way else up
        )

    def direct_in(k, way):
        zc = chunk(k)
        slot = normed.at[zc, yp if way else ym]
        return copy(slot, slot, y_send.at[k, way], y_recv.at[k, way], up)

    def forward(k, way):
        zc = chunk(k)
        slot = normed.at[zc, yp if way else ym, pl.ds(2 * way, 2)]
        return copy(slot, slot, y_send.at[k, 2 + way], y_recv.at[k, 2 + way], down if way else up)

    def forward_in(k, way):
        zc = chunk(k)
        slot = normed.at[zc, y2, pl.ds(2 * way, 2)]
        return copy(slot, slot, y_send.at[k, 2 + way], y_recv.at[k, 2 + way], up)

    def w_first(r):
        p = lax.rem(q + r, 8)
        slot = masked.at[z, own_j, xl]
        return copy(slot, slot, w_send.at[r], w_recv.at[r], dev(z, lax.div(p, 2), lax.rem(p, 2), y))

    def w_first_in(r):
        p = lax.rem(q + 8 - r, 8)
        px, pc = lax.div(p, 2), lax.rem(p, 2)
        slot = masked.at[z, lax.div(px, 2) * 2 + pc, lax.rem(px, 2)]
        return copy(slot, slot, w_send.at[r], w_recv.at[r], sibling)

    def w_ring(offset, to, at_receiver):
        slot = masked.at[lax.rem(z + offset, NZ), pl.ds(2 * c, 2)]
        return copy(slot, slot, wz_send.at[at_receiver], wz_recv.at[at_receiver], dev(to, x, c, y))

    def w_ring_in(offset):
        return w_ring(offset, zp, offset)

    def w_share(offset):
        slot = masked.at[lax.rem(z + offset, NZ), pl.ds(2 * c, 2)]
        return copy(slot, slot, wd_send.at[offset], wd_recv.at[offset], sibling)

    def w_share_in(offset):
        slot = masked.at[lax.rem(z + offset, NZ), pl.ds(2 * (1 - c), 2)]
        return copy(slot, slot, wd_send.at[offset], wd_recv.at[offset], sibling)

    def cot_swap():
        src = cot.at[pl.ds(pl.multiple_of((1 - xl) * group, group), group)]
        return copy(src, cot_in, o_send.at[0], o_recv.at[0], beside)

    def proj_swap():
        return copy(p_out, p_in, o_send.at[1], o_recv.at[1], beside)

    def core_swap(k):
        return copy(
            part.at[lax.rem(k, 2), pl.ds(0, 2)], core_in.at[k], c_send.at[k], c_recv.at[k], sibling
        )

    def x_term(k, d):
        xd = lax.rem(x + d, NX)
        return copy(
            x_out.at[k, d - 1], x_in.at[k, d - 1], x_send.at[k, d - 1], x_recv.at[k, d - 1], dev(z, xd, c, y)
        )

    def z_term(k):
        return copy(z_out.at[k], z_in.at[k], z_send.at[k], z_recv.at[k], dev(chunk(k), x, c, y))

    normalize(0)
    pl.semaphore_wait(barrier, 16)
    for k in range(2):
        if k:
            normalize(k)
        direct(k, 0).start()
        direct(k, 1).start()
        if k == 0:
            for r in range(1, 8):
                w_first(r).start()
            cot_swap().start()

    acc[...] = jnp.zeros_like(acc)
    mine = cot[pl.ds(pl.multiple_of(xl * group, group), group), :]
    cot_t[pl.ds(0, side), :] = mine.T
    cot_swap().wait_recv()
    cot_t[pl.ds(side, side), :] = cot_in[...].T

    for r in range(1, 8):
        w_first_in(r).wait_recv()
    w_ring(0, zp, 7).start()
    w_ring(0, zm, 1).start()

    def products(k, other, first):
        zc, slot = chunk(k), lax.rem(k, 2)

        @pl.loop(0, 2)
        def _(h):
            j = h * 2 + other
            n = normed[zc, :, j].reshape(group, side)
            d = jnp.dot(cot_t[...], n, preferred_element_type=jnp.float32)
            part[slot, first + h] = d.reshape(2, side, side)
            for u in range(2):
                w = masked[zc, j, lax.rem(xl + u, 2)]
                acc[u] += jnp.dot(n, w, preferred_element_type=jnp.float32)

    @pl.loop(0, NZ + 3)
    def _(i):
        @pl.when(i < NZ)
        def _():
            for way in range(2):
                direct_in(i, way).wait_recv()
                forward(i, way).start()
            for way in range(2):
                direct(i, way).wait_send()

            @pl.when(i < NZ - 2)
            def _():
                normalize(i + 2)
                direct(i + 2, 0).start()
                direct(i + 2, 1).start()

        @pl.when(i < 4)
        def _():
            w_ring_in(7 - i).wait_recv()
            w_share(7 - i).start()

            @pl.when(i < 3)
            def _():
                w_ring(7 - i, zp, 6 - i).start()
                w_ring_in(i + 1).wait_recv()
                w_share(i + 1).start()

            @pl.when(i < 2)
            def _():
                w_ring(i + 1, zm, i + 2).start()

        @pl.when((i >= 1) & (i <= NZ))
        def _():
            k = i - 1
            forward_in(k, 0).wait_recv()
            forward_in(k, 1).wait_recv()

            @pl.when(k < NZ - 1)
            def _():
                w_share_in(k + 1).wait_recv()

            @pl.when(k >= 2)
            def _():
                core_swap(k - 2).wait_send()

            products(k, 1 - c, 0)
            core_swap(k).start()
            products(k, c, 2)

            @pl.when(k == NZ - 1)
            def _():
                p_out[...] = acc[1].astype(jnp.bfloat16)
                proj_swap().start()

        @pl.when((i >= 2) & (i <= NZ + 1))
        def _():
            k = i - 2
            slot = lax.rem(k, 2)
            core_swap(k).wait_recv()
            for d in range(1, NX):
                xd = lax.rem(x + d, NX)
                h, u = lax.div(xd, 2), lax.rem(xd + xl, 2)
                x_out[k, d - 1] = (part[slot, 2 + h, u] + core_in[k, h, u]).astype(jnp.bfloat16)
                x_term(k, d).start()
            keep[slot] = part[slot, 2 + xh, 0] + core_in[k, xh, 0]

        @pl.when(i >= 3)
        def _():
            k = i - 3
            slot = lax.rem(k, 2)
            for d in range(1, NX):
                x_term(k, d).wait_recv()
            terms = [x_in[k, d].astype(jnp.float32) for d in range(NX - 1)]
            total = keep[slot] + (terms[0] + terms[1] + terms[2])

            @pl.when(k < NZ - 1)
            def _():
                z_out[k] = total
                z_term(k).start()

            @pl.when(k == NZ - 1)
            def _():
                keep[slot] = total

    for k in range(NZ - 1):
        z_term(k).wait_recv()
    total = keep[(NZ - 1) % 2]
    for k in range(NZ - 1):
        total = total + z_in[k]
    total = total.T
    for a in range(side // BLOCK):
        for b in range(side // BLOCK):
            m = mask[a, b].astype(jnp.float32)
            grad[pl.ds(a * BLOCK, BLOCK), pl.ds(b * BLOCK, BLOCK)] = (
                total[a * BLOCK : (a + 1) * BLOCK, b * BLOCK : (b + 1) * BLOCK] * m
            )

    proj[pl.ds(pl.multiple_of(xl * group, group), group), :] = acc[0].astype(jnp.bfloat16)
    proj_swap().wait_recv()
    proj[pl.ds(pl.multiple_of((1 - xl) * group, group), group), :] = p_in[...]

    @pl.loop(0, NZ)
    def _(k):
        forward(k, 0).wait_send()
        forward(k, 1).wait_send()
        for d in range(1, NX):
            x_term(k, d).wait_send()

    @pl.loop(0, NZ - 1)
    def _(k):
        w_first(k + 1).wait_send()
        w_ring_in(k + 1).wait_send()
        w_share(k + 1).wait_send()
        z_term(k).wait_send()

    core_swap(NZ - 2).wait_send()
    core_swap(NZ - 1).wait_send()
    cot_swap().wait_send()
    proj_swap().wait_send()


def per_device(tokens, gain, kv_weight, block_mask, cotangent):
    rows, width = tokens.shape
    side = kv_weight.shape[0]
    group = NY * rows
    bf16, f32 = jnp.bfloat16, jnp.float32
    dma = pltpu.SemaphoreType.DMA
    vmem = pl.BlockSpec(memory_space=pltpu.VMEM)
    pairs = [(NZ, 4), (8,), (NZ,), (NZ,), (NZ,), (NZ, 3), (NZ,), (2,)]
    return pl.pallas_call(
        kernel,
        out_shape=(
            jax.ShapeDtypeStruct(cotangent.shape, bf16),
            jax.ShapeDtypeStruct(kv_weight.shape, f32),
        ),
        in_specs=[vmem, vmem, vmem, pl.BlockSpec(memory_space=pltpu.SMEM), vmem],
        out_specs=(vmem, vmem),
        scratch_shapes=[
            pltpu.VMEM((NZ, NY, 4, rows, side), bf16),
            pltpu.VMEM((rows, side), f32),
            pltpu.VMEM((NZ, 4, 2, side, side), bf16),
            pltpu.VMEM((group, side), bf16),
            pltpu.VMEM((2 * side, group), bf16),
            pltpu.VMEM((2, 4, 2, side, side), f32),
            pltpu.VMEM((NZ, 2, 2, side, side), f32),
            pltpu.VMEM((2, side, side), f32),
            pltpu.VMEM((NZ, NX - 1, side, side), bf16),
            pltpu.VMEM((NZ, NX - 1, side, side), bf16),
            pltpu.VMEM((NZ - 1, side, side), f32),
            pltpu.VMEM((NZ - 1, side, side), f32),
            pltpu.VMEM((2, group, side), f32),
            pltpu.VMEM((group, side), bf16),
            pltpu.VMEM((group, side), bf16),
        ]
        + [dma(shape) for shape in pairs for _ in range(2)],
        compiler_params=pltpu.CompilerParams(
            collective_id=0, has_side_effects=True, vmem_limit_bytes=60 * 1024 * 1024
        ),
        cost_estimate=pl.CostEstimate(
            flops=8 * group * width * side, bytes_accessed=2 * rows * width, transcendentals=rows
        ),
    )(tokens, gain.reshape(1, width), kv_weight, block_mask, cotangent)


def solution(mesh):
    return jax.shard_map(
        per_device,
        mesh=mesh,
        in_specs=(
            P(("fsdp", "tensor"), None),
            P(),
            P("fsdp", "tensor"),
            P("fsdp", "tensor"),
            P("fsdp", "tensor"),
        ),
        out_specs=(P("fsdp", "tensor"), P("fsdp", "tensor")),
        check_vma=False,
    )
```

```python
import jax
import jax.numpy as jnp
from jax import lax
from jax.experimental import pallas as pl
from jax.experimental.pallas import tpu as pltpu
from jax.sharding import PartitionSpec as P

MESH = pl.DeviceIdType.MESH
NZ, NX, NC, NY = 8, 4, 2, 4
BLOCK = 128
AHEAD = 3


def kernel(
    tokens, gain, weight, mask, cot, proj, grad,
    normed, scale, masked, cot_in, cot_t, part, core_in, keep, x_out, x_in,
    z_out, z_in, acc, p_out, p_in,
    y_send, y_recv, w_send, w_recv, wz_send, wz_recv, wd_send, wd_recv,
    c_send, c_recv, x_send, x_recv, z_send, z_recv, o_send, o_recv,
):
    rows = tokens.shape[0]
    group = NY * rows
    side = weight.shape[0]
    wide = 4 * side
    steps = 2 * NZ
    f, t = lax.axis_index("fsdp"), lax.axis_index("tensor")
    z, xh, c = lax.div(f, 4), lax.rem(lax.div(f, 2), 2), lax.rem(f, 2)
    xl, y = lax.div(t, NY), lax.rem(t, NY)
    x = xh * 2 + xl
    q = x * 2 + c
    yp, ym, y2 = lax.rem(y + 1, NY), lax.rem(y + 3, NY), lax.rem(y + 2, NY)
    zp, zm = lax.rem(z + 1, NZ), lax.rem(z + NZ - 1, NZ)

    def dev(zz, xx, cc, yy):
        return ((zz * 2 + lax.div(xx, 2)) * 2 + cc, lax.rem(xx, 2) * NY + yy)

    def chunk(m):
        return lax.rem(z + 1 + m, NZ)

    def half(k):
        return chunk(lax.div(k, 2)), lax.rem(xh + 1 + k, 2)

    def copy(src, dst, send, recv, to):
        return pltpu.make_async_remote_copy(
            src_ref=src, dst_ref=dst, send_sem=send, recv_sem=recv, device_id=to, device_id_type=MESH
        )

    sibling = dev(z, x, 1 - c, y)
    beside = dev(z, xh * 2 + 1 - xl, c, y)
    up, down = dev(z, x, c, yp), dev(z, x, c, ym)

    barrier = pltpu.get_barrier_semaphore()

    def greet(to):
        pl.semaphore_signal(barrier, inc=1, device_id=to, device_id_type=MESH)

    greet(up)
    greet(down)
    for r in range(1, 8):
        p = lax.rem(q + r, 8)
        greet(dev(z, lax.div(p, 2), lax.rem(p, 2), y))
        greet(dev(lax.rem(z + r, NZ), x, c, y))

    own_j = xh * 2 + c
    for a in range(side // BLOCK):
        for b in range(side // BLOCK):
            at = (pl.ds(a * BLOCK, BLOCK), pl.ds(b * BLOCK, BLOCK))
            m = mask[a, b].astype(jnp.float32)
            masked[z, own_j, xl, at[0], at[1]] = (weight[at].astype(jnp.float32) * m).astype(jnp.bfloat16)

    @pl.loop(0, rows // 16)
    def _(r):
        at = pl.ds(pl.multiple_of(r * 16, 16), 16)
        v = tokens[at, :].astype(jnp.float32)
        square = jnp.mean(v * v, axis=-1, keepdims=True)
        scale[at, :] = jnp.broadcast_to(lax.rsqrt(square + 1e-05), (16, side))

    def normalize(k):
        zc, h = half(k)

        @pl.loop(0, 2)
        def _(e):
            at = pl.ds(pl.multiple_of(zc * wide + (2 * h + e) * side, side), side)
            v = tokens[:, at].astype(jnp.float32)
            g = gain[at].astype(jnp.float32).reshape(1, side)
            normed[zc, y, 2 * h + e] = (v * scale[...] * g).astype(jnp.bfloat16)

    def direct(k, way):
        zc, h = half(k)
        slot = normed.at[zc, y, pl.ds(2 * h, 2)]
        return copy(slot, slot, y_send.at[k, way], y_recv.at[k, way], down if way else up)

    def direct_in(k, way):
        zc, h = half(k)
        slot = normed.at[zc, yp if way else ym, pl.ds(2 * h, 2)]
        return copy(slot, slot, y_send.at[k, way], y_recv.at[k, way], up)

    def forward(k, way):
        zc, h = half(k)
        slot = normed.at[zc, yp if way else ym, 2 * h + way]
        return copy(slot, slot, y_send.at[k, 2 + way], y_recv.at[k, 2 + way], down if way else up)

    def forward_in(k, way):
        zc, h = half(k)
        slot = normed.at[zc, y2, 2 * h + way]
        return copy(slot, slot, y_send.at[k, 2 + way], y_recv.at[k, 2 + way], up)

    def w_first(r):
        p = lax.rem(q + r, 8)
        slot = masked.at[z, own_j, xl]
        return copy(slot, slot, w_send.at[r], w_recv.at[r], dev(z, lax.div(p, 2), lax.rem(p, 2), y))

    def w_first_in(r):
        p = lax.rem(q + 8 - r, 8)
        px, pc = lax.div(p, 2), lax.rem(p, 2)
        slot = masked.at[z, lax.div(px, 2) * 2 + pc, lax.rem(px, 2)]
        return copy(slot, slot, w_send.at[r], w_recv.at[r], sibling)

    def w_ring(offset, to, at_receiver):
        slot = masked.at[lax.rem(z + offset, NZ), pl.ds(2 * c, 2)]
        return copy(slot, slot, wz_send.at[at_receiver], wz_recv.at[at_receiver], dev(to, x, c, y))

    def w_ring_in(offset):
        return w_ring(offset, zp, offset)

    def w_share(offset):
        slot = masked.at[lax.rem(z + offset, NZ), pl.ds(2 * c, 2)]
        return copy(slot, slot, wd_send.at[offset], wd_recv.at[offset], sibling)

    def w_share_in(offset):
        slot = masked.at[lax.rem(z + offset, NZ), pl.ds(2 * (1 - c), 2)]
        return copy(slot, slot, wd_send.at[offset], wd_recv.at[offset], sibling)

    def cot_swap():
        src = cot.at[pl.ds(pl.multiple_of((1 - xl) * group, group), group)]
        return copy(src, cot_in, o_send.at[NY], o_recv.at[NY], beside)

    def proj_swap(away):
        at = lax.rem(y + away, NY)
        return copy(p_out.at[at], p_in.at[at], o_send.at[away], o_recv.at[away], beside)

    def core_swap(k):
        return copy(part.at[lax.rem(k, 2), 0], core_in.at[k], c_send.at[k], c_recv.at[k], sibling)

    def x_term(m, d):
        to = dev(z, (xh if d == 2 else 1 - xh) * 2 + (1 - xl if d else xl), c, y)
        return copy(x_out.at[m, d], x_in.at[m, d], x_send.at[m, d], x_recv.at[m, d], to)

    def z_term(m):
        return copy(z_out.at[m], z_in.at[m], z_send.at[m], z_recv.at[m], dev(chunk(m), x, c, y))

    def send(k):
        direct(k, 0).start()
        direct(k, 1).start()

    def relay(k):
        for way in range(2):
            direct_in(k, way).wait_recv()
            forward(k, way).start()

    def products(k):
        zc, h = half(k)
        slot = lax.rem(k, 2)
        forward_in(k, 0).wait_recv()
        forward_in(k, 1).wait_recv()
        for own in range(2):
            n = normed[zc, :, 2 * h + (c if own else 1 - c)].reshape(group, side)
            d = jnp.dot(cot_t[...], n, preferred_element_type=jnp.float32)
            part[slot, own] = d.reshape(2, side, side)
            if not own:
                core_swap(k).start()

    def add_cores(k, far):
        m, slot = lax.div(k, 2), lax.rem(k, 2)
        core_swap(k).wait()
        if far:
            for u in range(2):
                x_out[m, u] = (part[slot, 1, u] + core_in[k, u]).astype(jnp.bfloat16)
                x_term(m, u).start()
        else:
            x_out[m, 2] = (part[slot, 1, 1] + core_in[k, 1]).astype(jnp.bfloat16)
            x_term(m, 2).start()
            keep[lax.rem(m, 2)] = part[slot, 1, 0] + core_in[k, 0]

    def gradient_block(m):
        for d in range(3):
            x_term(m, d).wait_recv()
        terms = [x_in[m, d].astype(jnp.float32) for d in range(3)]
        return keep[lax.rem(m, 2)] + (terms[0] + terms[1] + terms[2])

    def project(m):
        zc = chunk(m)

        @pl.loop(0, 4)
        def _(j):
            n = normed[zc, :, j].reshape(group, side)
            for u in range(2):
                w = masked[zc, j, lax.rem(xl + u, 2)]
                d = jnp.dot(n, w, preferred_element_type=jnp.float32)
                acc[u] += d.reshape(NY, rows, side)

    def project_rows(k, at):
        zc, h = half(k)
        for e in range(2):
            n = normed[zc, at, 2 * h + e]
            for u in range(2):
                w = masked[zc, 2 * h + e, lax.rem(xl + u, 2)]
                acc[u, at] += jnp.dot(n, w, preferred_element_type=jnp.float32)

    normalize(0)
    pl.semaphore_wait(barrier, 16)
    send(0)
    for r in range(1, 8):
        w_first(r).start()
    cot_swap().start()
    for k in range(1, AHEAD):
        normalize(k)
        send(k)

    acc[...] = jnp.zeros_like(acc)
    mine = cot[pl.ds(pl.multiple_of(xl * group, group), group), :]
    cot_t[pl.ds(0, side), :] = mine.T

    @pl.loop(0, NZ)
    def _(m):
        for e in range(2):
            k = 2 * m + e
            relay(k)
            for way in range(2):
                direct(k, way).wait_send()

            @pl.when(k < steps - AHEAD)
            def _():
                normalize(k + AHEAD)
                send(k + AHEAD)

            if e == 0:

                @pl.when(m == 1)
                def _():
                    cot_swap().wait_recv()
                    cot_t[pl.ds(side, side), :] = cot_in[...].T

                @pl.when((m >= 2) & (m <= 5))
                def _():
                    hop = m - 1
                    w_ring_in(8 - hop).wait_recv()
                    w_share(8 - hop).start()

                    @pl.when(hop < 4)
                    def _():
                        w_ring(8 - hop, zp, 7 - hop).start()
                        w_ring_in(hop).wait_recv()
                        w_share(hop).start()

                    @pl.when(hop < 3)
                    def _():
                        w_ring(hop, zm, hop + 1).start()

                @pl.when(m >= 3)
                def _():
                    z_out[m - 3] = gradient_block(m - 3).astype(z_out.dtype)
                    z_term(m - 3).start()

                @pl.when(m >= 2)
                def _():
                    add_cores(k - 3, False)

                @pl.when(m >= 1)
                def _():
                    products(k - 2)

                @pl.when(m == NZ - 1)
                def _():
                    w_share_in(NZ - 2).wait_recv()
                    project(NZ - 3)
                    w_share_in(NZ - 1).wait_recv()
                    for n in range(-2, 2):
                        project_rows(k + n, y)
                    p_out[y] = acc[1, y].astype(jnp.bfloat16)
                    proj_swap(0).start()

            else:

                @pl.when(m == 0)
                def _():
                    for r in range(1, 8):
                        w_first_in(r).wait_recv()
                    w_ring(0, zp, 7).start()
                    w_ring(0, zm, 1).start()

                @pl.when((m >= 2) & (m < NZ - 1))
                def _():
                    w_share_in(m - 1).wait_recv()
                    project(m - 2)

                @pl.when(m == NZ - 1)
                def _():
                    z_out[NZ - 3] = gradient_block(NZ - 3).astype(z_out.dtype)
                    z_term(NZ - 3).start()

                @pl.when(m >= 1)
                def _():
                    add_cores(k - 3, True)

                @pl.when(m == NZ - 1)
                def _():
                    for away in (1, 3):
                        at = lax.rem(y + away, NY)
                        for n in range(-3, 1):
                            project_rows(k + n, at)
                        p_out[at] = acc[1, at].astype(jnp.bfloat16)
                        proj_swap(away).start()

                @pl.when(m >= 1)
                def _():
                    products(k - 2)

    last = steps - 1
    products(last - 1)
    add_cores(last - 2, False)
    products(last)
    add_cores(last - 1, True)
    for k in range(last - 3, last + 1):
        project_rows(k, y2)
    p_out[y2] = acc[1, y2].astype(jnp.bfloat16)
    add_cores(last, False)
    proj_swap(2).start()
    z_out[NZ - 2] = gradient_block(NZ - 2).astype(z_out.dtype)
    z_term(NZ - 2).start()
    proj[pl.ds(pl.multiple_of(xl * group, group), group), :] = acc[0].reshape(group, side).astype(jnp.bfloat16)

    total = gradient_block(NZ - 1)
    for m in range(NZ - 1):
        z_term(m).wait_recv()
        total = total + z_in[m].astype(jnp.float32)
    total = total.T
    for a in range(side // BLOCK):
        for b in range(side // BLOCK):
            m = mask[a, b].astype(jnp.float32)
            grad[pl.ds(a * BLOCK, BLOCK), pl.ds(b * BLOCK, BLOCK)] = (
                total[a * BLOCK : (a + 1) * BLOCK, b * BLOCK : (b + 1) * BLOCK] * m
            )

    for away in (0, 1, 3, 2):
        proj_swap(away).wait_recv()
    proj[pl.ds(pl.multiple_of((1 - xl) * group, group), group), :] = p_in[...].reshape(group, side)

    @pl.loop(0, steps)
    def _(k):
        forward(k, 0).wait_send()
        forward(k, 1).wait_send()

    @pl.loop(0, NZ)
    def _(m):
        for d in range(3):
            x_term(m, d).wait_send()

    @pl.loop(0, NZ - 1)
    def _(m):
        w_first(m + 1).wait_send()
        w_ring_in(m + 1).wait_send()
        w_share(m + 1).wait_send()
        z_term(m).wait_send()

    cot_swap().wait_send()
    for away in range(NY):
        proj_swap(away).wait_send()


def per_device(tokens, gain, kv_weight, block_mask, cotangent):
    rows, width = tokens.shape
    side = kv_weight.shape[0]
    group = NY * rows
    bf16, f32 = jnp.bfloat16, jnp.float32
    dma = pltpu.SemaphoreType.DMA
    vmem = pl.BlockSpec(memory_space=pltpu.VMEM)
    pairs = [(2 * NZ, 4), (8,), (NZ,), (NZ,), (2 * NZ,), (NZ, 3), (NZ,), (NY + 1,)]
    return pl.pallas_call(
        kernel,
        out_shape=(
            jax.ShapeDtypeStruct(cotangent.shape, bf16),
            jax.ShapeDtypeStruct(kv_weight.shape, f32),
        ),
        in_specs=[vmem, vmem, vmem, pl.BlockSpec(memory_space=pltpu.SMEM), vmem],
        out_specs=(vmem, vmem),
        scratch_shapes=[
            pltpu.VMEM((NZ, NY, 4, rows, side), bf16),
            pltpu.VMEM((rows, side), f32),
            pltpu.VMEM((NZ, 4, 2, side, side), bf16),
            pltpu.VMEM((group, side), bf16),
            pltpu.VMEM((2 * side, group), bf16),
            pltpu.VMEM((2, 2, 2, side, side), f32),
            pltpu.VMEM((2 * NZ, 2, side, side), f32),
            pltpu.VMEM((2, side, side), f32),
            pltpu.VMEM((NZ, 3, side, side), bf16),
            pltpu.VMEM((NZ, 3, side, side), bf16),
            pltpu.VMEM((NZ - 1, side, side), bf16),
            pltpu.VMEM((NZ - 1, side, side), bf16),
            pltpu.VMEM((2, NY, rows, side), f32),
            pltpu.VMEM((NY, rows, side), bf16),
            pltpu.VMEM((NY, rows, side), bf16),
        ]
        + [dma(shape) for shape in pairs for _ in range(2)],
        compiler_params=pltpu.CompilerParams(
            collective_id=0, has_side_effects=True, vmem_limit_bytes=60 * 1024 * 1024
        ),
        cost_estimate=pl.CostEstimate(
            flops=8 * group * width * side, bytes_accessed=2 * rows * width, transcendentals=rows
        ),
    )(tokens, gain, kv_weight, block_mask, cotangent)


def solution(mesh):
    return jax.shard_map(
        per_device,
        mesh=mesh,
        in_specs=(
            P(("fsdp", "tensor"), None),
            P(),
            P("fsdp", "tensor"),
            P("fsdp", "tensor"),
            P("fsdp", "tensor"),
        ),
        out_specs=(P("fsdp", "tensor"), P("fsdp", "tensor")),
        check_vma=False,
    )
```

```python
import jax
import jax.numpy as jnp
from jax import lax
from jax.experimental import pallas as pl
from jax.experimental.pallas import tpu as pltpu
from jax.sharding import PartitionSpec as P

MESH = pl.DeviceIdType.MESH
NZ, NX, NC, NY = 8, 4, 2, 4
BLOCK = 128
AHEAD = 3


def kernel(
    tokens_in, gain, weight, mask, cot, proj, grad,
    tokens, normed, scale, masked, cot_in, cot_t, part, core_in, keep, x_out, x_in,
    z_out, z_in, acc, p_out, p_in,
    y_send, y_recv, w_send, w_recv, wz_send, wz_recv, wd_send, wd_recv,
    c_send, c_recv, x_send, x_recv, z_send, z_recv, o_send, o_recv, load_sem,
):
    rows = tokens.shape[0]
    group = NY * rows
    side = weight.shape[0]
    wide = 4 * side
    steps = 2 * NZ
    f, t = lax.axis_index("fsdp"), lax.axis_index("tensor")
    z, xh, c = lax.div(f, 4), lax.rem(lax.div(f, 2), 2), lax.rem(f, 2)
    xl, y = lax.div(t, NY), lax.rem(t, NY)
    x = xh * 2 + xl
    q = x * 2 + c
    yp, ym, y2 = lax.rem(y + 1, NY), lax.rem(y + 3, NY), lax.rem(y + 2, NY)
    zp, zm = lax.rem(z + 1, NZ), lax.rem(z + NZ - 1, NZ)

    def dev(zz, xx, cc, yy):
        return ((zz * 2 + lax.div(xx, 2)) * 2 + cc, lax.rem(xx, 2) * NY + yy)

    def chunk(m):
        return lax.rem(z + 1 + m, NZ)

    def half(k):
        return chunk(lax.div(k, 2)), lax.rem(xh + 1 + k, 2)

    def copy(src, dst, send, recv, to):
        return pltpu.make_async_remote_copy(
            src_ref=src, dst_ref=dst, send_sem=send, recv_sem=recv, device_id=to, device_id_type=MESH
        )

    sibling = dev(z, x, 1 - c, y)
    beside = dev(z, xh * 2 + 1 - xl, c, y)
    up, down = dev(z, x, c, yp), dev(z, x, c, ym)

    quarter = rows // 4

    def load(n):
        at = pl.ds(n * quarter, quarter)
        return pltpu.make_async_copy(tokens_in.at[at], tokens.at[at], load_sem.at[n])

    for n in range(4):
        load(n).start()

    barrier = pltpu.get_barrier_semaphore()

    def greet(to):
        pl.semaphore_signal(barrier, inc=1, device_id=to, device_id_type=MESH)

    greet(up)
    greet(down)
    for r in range(1, 8):
        p = lax.rem(q + r, 8)
        greet(dev(z, lax.div(p, 2), lax.rem(p, 2), y))
        greet(dev(lax.rem(z + r, NZ), x, c, y))

    own_j = xh * 2 + c
    for a in range(side // BLOCK):
        for b in range(side // BLOCK):
            at = (pl.ds(a * BLOCK, BLOCK), pl.ds(b * BLOCK, BLOCK))
            m = mask[a, b].astype(jnp.float32)
            masked[z, own_j, xl, at[0], at[1]] = (weight[at].astype(jnp.float32) * m).astype(jnp.bfloat16)

    for n in range(4):
        load(n).wait()

        @pl.loop(n * quarter // 16, (n + 1) * quarter // 16)
        def _(r):
            at = pl.ds(pl.multiple_of(r * 16, 16), 16)
            v = tokens[at, :].astype(jnp.float32)
            square = jnp.mean(v * v, axis=-1, keepdims=True)
            scale[at, :] = jnp.broadcast_to(lax.rsqrt(square + 1e-05), (16, side))

    def normalize(k):
        zc, h = half(k)

        @pl.loop(0, 2)
        def _(e):
            at = pl.ds(pl.multiple_of(zc * wide + (2 * h + e) * side, side), side)
            v = tokens[:, at].astype(jnp.float32)
            g = gain[at].astype(jnp.float32).reshape(1, side)
            normed[zc, y, 2 * h + e] = (v * scale[...] * g).astype(jnp.bfloat16)

    def direct(k, way):
        zc, h = half(k)
        slot = normed.at[zc, y, pl.ds(2 * h, 2)]
        return copy(slot, slot, y_send.at[k, way], y_recv.at[k, way], down if way else up)

    def direct_in(k, way):
        zc, h = half(k)
        slot = normed.at[zc, yp if way else ym, pl.ds(2 * h, 2)]
        return copy(slot, slot, y_send.at[k, way], y_recv.at[k, way], up)

    def forward(k, way):
        zc, h = half(k)
        slot = normed.at[zc, yp if way else ym, 2 * h + way]
        return copy(slot, slot, y_send.at[k, 2 + way], y_recv.at[k, 2 + way], down if way else up)

    def forward_in(k, way):
        zc, h = half(k)
        slot = normed.at[zc, y2, 2 * h + way]
        return copy(slot, slot, y_send.at[k, 2 + way], y_recv.at[k, 2 + way], up)

    def w_first(r):
        p = lax.rem(q + r, 8)
        slot = masked.at[z, own_j, xl]
        return copy(slot, slot, w_send.at[r], w_recv.at[r], dev(z, lax.div(p, 2), lax.rem(p, 2), y))

    def w_first_in(r):
        p = lax.rem(q + 8 - r, 8)
        px, pc = lax.div(p, 2), lax.rem(p, 2)
        slot = masked.at[z, lax.div(px, 2) * 2 + pc, lax.rem(px, 2)]
        return copy(slot, slot, w_send.at[r], w_recv.at[r], sibling)

    def w_ring(offset, to, at_receiver):
        slot = masked.at[lax.rem(z + offset, NZ), pl.ds(2 * c, 2)]
        return copy(slot, slot, wz_send.at[at_receiver], wz_recv.at[at_receiver], dev(to, x, c, y))

    def w_ring_in(offset):
        return w_ring(offset, zp, offset)

    def w_share(offset):
        slot = masked.at[lax.rem(z + offset, NZ), pl.ds(2 * c, 2)]
        return copy(slot, slot, wd_send.at[offset], wd_recv.at[offset], sibling)

    def w_share_in(offset):
        slot = masked.at[lax.rem(z + offset, NZ), pl.ds(2 * (1 - c), 2)]
        return copy(slot, slot, wd_send.at[offset], wd_recv.at[offset], sibling)

    def cot_swap():
        src = cot.at[pl.ds(pl.multiple_of((1 - xl) * group, group), group)]
        return copy(src, cot_in, o_send.at[NY], o_recv.at[NY], beside)

    def proj_swap(away):
        at = lax.rem(y + away, NY)
        return copy(p_out.at[at], p_in.at[at], o_send.at[away], o_recv.at[away], beside)

    def core_swap(k):
        return copy(part.at[lax.rem(k, 2), 0], core_in.at[k], c_send.at[k], c_recv.at[k], sibling)

    def x_term(m, d):
        to = dev(z, (xh if d == 2 else 1 - xh) * 2 + (1 - xl if d else xl), c, y)
        return copy(x_out.at[m, d], x_in.at[m, d], x_send.at[m, d], x_recv.at[m, d], to)

    def z_term(m):
        return copy(z_out.at[m], z_in.at[m], z_send.at[m], z_recv.at[m], dev(chunk(m), x, c, y))

    def send(k):
        direct(k, 0).start()
        direct(k, 1).start()

    def relay(k):
        for way in range(2):
            direct_in(k, way).wait_recv()
            forward(k, way).start()

    def products(k):
        zc, h = half(k)
        slot = lax.rem(k, 2)
        forward_in(k, 0).wait_recv()
        forward_in(k, 1).wait_recv()
        for own in range(2):
            n = normed[zc, :, 2 * h + (c if own else 1 - c)].reshape(group, side)
            d = jnp.dot(cot_t[...], n, preferred_element_type=jnp.float32)
            part[slot, own] = d.reshape(2, side, side)
            if not own:
                core_swap(k).start()

    def add_cores(k, far):
        m, slot = lax.div(k, 2), lax.rem(k, 2)
        core_swap(k).wait()
        if far:
            for u in range(2):
                x_out[m, u] = (part[slot, 1, u] + core_in[k, u]).astype(jnp.bfloat16)
                x_term(m, u).start()
        else:
            x_out[m, 2] = (part[slot, 1, 1] + core_in[k, 1]).astype(jnp.bfloat16)
            x_term(m, 2).start()
            keep[lax.rem(m, 2)] = part[slot, 1, 0] + core_in[k, 0]

    def gradient_block(m):
        for d in range(3):
            x_term(m, d).wait_recv()
        terms = [x_in[m, d].astype(jnp.float32) for d in range(3)]
        return keep[lax.rem(m, 2)] + (terms[0] + terms[1] + terms[2])

    def project(m):
        zc = chunk(m)

        @pl.loop(0, 4)
        def _(j):
            n = normed[zc, :, j].reshape(group, side)
            for u in range(2):
                w = masked[zc, j, lax.rem(xl + u, 2)]
                d = jnp.dot(n, w, preferred_element_type=jnp.float32)
                acc[u] += d.reshape(NY, rows, side)

    def project_rows(k, at):
        zc, h = half(k)
        for e in range(2):
            n = normed[zc, at, 2 * h + e]
            for u in range(2):
                w = masked[zc, 2 * h + e, lax.rem(xl + u, 2)]
                acc[u, at] += jnp.dot(n, w, preferred_element_type=jnp.float32)

    normalize(0)
    pl.semaphore_wait(barrier, 16)
    send(0)
    for r in range(1, 8):
        w_first(r).start()
    cot_swap().start()
    for k in range(1, AHEAD):
        normalize(k)
        send(k)

    acc[...] = jnp.zeros_like(acc)
    mine = cot[pl.ds(pl.multiple_of(xl * group, group), group), :]
    cot_t[pl.ds(0, side), :] = mine.T

    @pl.loop(0, NZ)
    def _(m):
        for e in range(2):
            k = 2 * m + e
            relay(k)
            for way in range(2):
                direct(k, way).wait_send()

            @pl.when(k < steps - AHEAD)
            def _():
                normalize(k + AHEAD)
                send(k + AHEAD)

            if e == 0:

                @pl.when(m == 1)
                def _():
                    cot_swap().wait_recv()
                    cot_t[pl.ds(side, side), :] = cot_in[...].T

                @pl.when((m >= 2) & (m <= 5))
                def _():
                    hop = m - 1
                    w_ring_in(8 - hop).wait_recv()
                    w_share(8 - hop).start()

                    @pl.when(hop < 4)
                    def _():
                        w_ring(8 - hop, zp, 7 - hop).start()
                        w_ring_in(hop).wait_recv()
                        w_share(hop).start()

                    @pl.when(hop < 3)
                    def _():
                        w_ring(hop, zm, hop + 1).start()

                @pl.when(m >= 3)
                def _():
                    z_out[m - 3] = gradient_block(m - 3).astype(z_out.dtype)
                    z_term(m - 3).start()

                @pl.when(m >= 2)
                def _():
                    add_cores(k - 3, False)

                @pl.when(m >= 1)
                def _():
                    products(k - 2)

                @pl.when(m == NZ - 1)
                def _():
                    for away in (1, 3):
                        for n in range(-4, 0):
                            project_rows(k + n, lax.rem(y + away, NY))

            else:

                @pl.when(m == 0)
                def _():
                    for r in range(1, 8):
                        w_first_in(r).wait_recv()
                    w_ring(0, zp, 7).start()
                    w_ring(0, zm, 1).start()

                @pl.when((m >= 2) & (m < NZ - 1))
                def _():
                    w_share_in(m - 1).wait_recv()
                    project(m - 2)

                @pl.when(m == NZ - 2)
                def _():
                    w_share_in(NZ - 2).wait_recv()
                    w_share_in(NZ - 1).wait_recv()
                    for n in range(-3, 3):
                        project_rows(k + n, y)
                    p_out[y] = acc[1, y].astype(jnp.bfloat16)
                    proj_swap(0).start()

                @pl.when(m == NZ - 1)
                def _():
                    z_out[NZ - 3] = gradient_block(NZ - 3).astype(z_out.dtype)
                    z_term(NZ - 3).start()

                @pl.when(m >= 1)
                def _():
                    add_cores(k - 3, True)

                @pl.when(m == NZ - 1)
                def _():
                    for away in (1, 3):
                        at = lax.rem(y + away, NY)
                        for n in range(-1, 1):
                            project_rows(k + n, at)
                        p_out[at] = acc[1, at].astype(jnp.bfloat16)
                        proj_swap(away).start()

                @pl.when(m >= 1)
                def _():
                    products(k - 2)

    last = steps - 1
    products(last - 1)
    add_cores(last - 2, False)
    for k in range(last - 5, last):
        project_rows(k, y2)
    add_cores(last - 1, True)
    products(last)
    add_cores(last, False)
    project_rows(last, y2)
    p_out[y2] = acc[1, y2].astype(jnp.bfloat16)
    proj_swap(2).start()
    z_out[NZ - 2] = gradient_block(NZ - 2).astype(z_out.dtype)
    z_term(NZ - 2).start()
    proj[pl.ds(pl.multiple_of(xl * group, group), group), :] = acc[0].reshape(group, side).astype(jnp.bfloat16)

    total = gradient_block(NZ - 1)
    for m in range(NZ - 1):
        z_term(m).wait_recv()
        total = total + z_in[m].astype(jnp.float32)
    total = total.T
    for a in range(side // BLOCK):
        for b in range(side // BLOCK):
            m = mask[a, b].astype(jnp.float32)
            grad[pl.ds(a * BLOCK, BLOCK), pl.ds(b * BLOCK, BLOCK)] = (
                total[a * BLOCK : (a + 1) * BLOCK, b * BLOCK : (b + 1) * BLOCK] * m
            )

    for away in (0, 1, 3, 2):
        proj_swap(away).wait_recv()
    proj[pl.ds(pl.multiple_of((1 - xl) * group, group), group), :] = p_in[...].reshape(group, side)

    @pl.loop(0, steps)
    def _(k):
        forward(k, 0).wait_send()
        forward(k, 1).wait_send()

    @pl.loop(0, NZ)
    def _(m):
        for d in range(3):
            x_term(m, d).wait_send()

    @pl.loop(0, NZ - 1)
    def _(m):
        w_first(m + 1).wait_send()
        w_ring_in(m + 1).wait_send()
        w_share(m + 1).wait_send()
        z_term(m).wait_send()

    cot_swap().wait_send()
    for away in range(NY):
        proj_swap(away).wait_send()


def hand_over(proj_in, grad_in, proj, grad):
    proj[...] = proj_in[...]
    grad[...] = grad_in[...]


def per_device(tokens, gain, kv_weight, block_mask, cotangent):
    rows, width = tokens.shape
    side = kv_weight.shape[0]
    group = NY * rows
    bf16, f32 = jnp.bfloat16, jnp.float32
    dma = pltpu.SemaphoreType.DMA
    vmem = pl.BlockSpec(memory_space=pltpu.VMEM)
    pairs = [(2 * NZ, 4), (8,), (NZ,), (NZ,), (2 * NZ,), (NZ, 3), (NZ,), (NY + 1,)]
    results = pl.pallas_call(
        kernel,
        out_shape=(
            jax.ShapeDtypeStruct(cotangent.shape, bf16),
            jax.ShapeDtypeStruct(kv_weight.shape, f32),
        ),
        in_specs=[pl.BlockSpec(memory_space=pl.ANY), vmem, vmem, pl.BlockSpec(memory_space=pltpu.SMEM), vmem],
        out_specs=(vmem, vmem),
        scratch_shapes=[
            pltpu.VMEM((rows, width), bf16),
            pltpu.VMEM((NZ, NY, 4, rows, side), bf16),
            pltpu.VMEM((rows, side), f32),
            pltpu.VMEM((NZ, 4, 2, side, side), bf16),
            pltpu.VMEM((group, side), bf16),
            pltpu.VMEM((2 * side, group), bf16),
            pltpu.VMEM((2, 2, 2, side, side), f32),
            pltpu.VMEM((2 * NZ, 2, side, side), f32),
            pltpu.VMEM((2, side, side), f32),
            pltpu.VMEM((NZ, 3, side, side), bf16),
            pltpu.VMEM((NZ, 3, side, side), bf16),
            pltpu.VMEM((NZ - 1, side, side), bf16),
            pltpu.VMEM((NZ - 1, side, side), bf16),
            pltpu.VMEM((2, NY, rows, side), f32),
            pltpu.VMEM((NY, rows, side), bf16),
            pltpu.VMEM((NY, rows, side), bf16),
        ]
        + [dma(shape) for shape in pairs for _ in range(2)]
        + [dma((4,))],
        compiler_params=pltpu.CompilerParams(
            collective_id=0, has_side_effects=True, vmem_limit_bytes=60 * 1024 * 1024
        ),
        cost_estimate=pl.CostEstimate(
            flops=8 * group * width * side, bytes_accessed=2 * rows * width, transcendentals=rows
        ),
    )(tokens, gain, kv_weight, block_mask, cotangent)
    return pl.pallas_call(
        hand_over,
        out_shape=tuple(jax.ShapeDtypeStruct(r.shape, r.dtype) for r in results),
        in_specs=[vmem] * 2,
        out_specs=(vmem,) * 2,
    )(*results)


def solution(mesh):
    return jax.shard_map(
        per_device,
        mesh=mesh,
        in_specs=(
            P(("fsdp", "tensor"), None),
            P(),
            P("fsdp", "tensor"),
            P("fsdp", "tensor"),
            P("fsdp", "tensor"),
        ),
        out_specs=(P("fsdp", "tensor"), P("fsdp", "tensor")),
        check_vma=False,
    )
```

```python
import jax
import jax.numpy as jnp
from jax import lax
from jax.experimental import pallas as pl
from jax.experimental.pallas import tpu as pltpu
from jax.sharding import PartitionSpec as P

MESH = pl.DeviceIdType.MESH
NZ, NX, NC, NY = 8, 4, 2, 4
BLOCK = 128
AHEAD = 3


def kernel(
    tokens_in, gain, weight, mask, cot, proj, grad,
    tokens, normed, scale, masked, cot_in, cot_t, part, core_in, keep, x_out, x_in,
    z_out, z_in, acc, p_out, p_in,
    y_send, y_recv, w_send, w_recv, wz_send, wz_recv, wd_send, wd_recv,
    c_send, c_recv, x_send, x_recv, z_send, z_recv, o_send, o_recv, load_sem,
):
    rows = tokens.shape[0]
    group = NY * rows
    side = weight.shape[0]
    wide = 4 * side
    steps = 2 * NZ
    f, t = lax.axis_index("fsdp"), lax.axis_index("tensor")
    z, xh, c = lax.div(f, 4), lax.rem(lax.div(f, 2), 2), lax.rem(f, 2)
    xl, y = lax.div(t, NY), lax.rem(t, NY)
    x = xh * 2 + xl
    q = x * 2 + c
    yp, ym, y2 = lax.rem(y + 1, NY), lax.rem(y + 3, NY), lax.rem(y + 2, NY)
    zp, zm = lax.rem(z + 1, NZ), lax.rem(z + NZ - 1, NZ)

    def dev(zz, xx, cc, yy):
        return ((zz * 2 + lax.div(xx, 2)) * 2 + cc, lax.rem(xx, 2) * NY + yy)

    def chunk(m):
        return lax.rem(z + 1 + m, NZ)

    def half(k):
        return chunk(lax.div(k, 2)), lax.rem(xh + 1 + k, 2)

    def copy(src, dst, send, recv, to):
        return pltpu.make_async_remote_copy(
            src_ref=src, dst_ref=dst, send_sem=send, recv_sem=recv, device_id=to, device_id_type=MESH
        )

    sibling = dev(z, x, 1 - c, y)
    beside = dev(z, xh * 2 + 1 - xl, c, y)
    up, down = dev(z, x, c, yp), dev(z, x, c, ym)

    quarter = rows // 4

    def load(n):
        at = pl.ds(n * quarter, quarter)
        return pltpu.make_async_copy(tokens_in.at[at], tokens.at[at], load_sem.at[n])

    for n in range(4):
        load(n).start()

    barrier = pltpu.get_barrier_semaphore()

    def greet(to):
        pl.semaphore_signal(barrier, inc=1, device_id=to, device_id_type=MESH)

    greet(up)
    greet(down)
    for r in range(1, 8):
        p = lax.rem(q + r, 8)
        greet(dev(z, lax.div(p, 2), lax.rem(p, 2), y))
        greet(dev(lax.rem(z + r, NZ), x, c, y))

    own_j = xh * 2 + c
    for a in range(side // BLOCK):
        for b in range(side // BLOCK):
            at = (pl.ds(a * BLOCK, BLOCK), pl.ds(b * BLOCK, BLOCK))
            m = mask[a, b].astype(jnp.float32)
            masked[z, own_j, xl, at[0], at[1]] = (weight[at].astype(jnp.float32) * m).astype(jnp.bfloat16)

    for n in range(4):
        load(n).wait()

        @pl.loop(n * quarter // 16, (n + 1) * quarter // 16)
        def _(r):
            at = pl.ds(pl.multiple_of(r * 16, 16), 16)
            v = tokens[at, :].astype(jnp.float32)
            square = jnp.mean(v * v, axis=-1, keepdims=True)
            scale[at, :] = jnp.broadcast_to(lax.rsqrt(square + 1e-05), (16, side))

    def normalize(k):
        zc, h = half(k)

        @pl.loop(0, 2)
        def _(e):
            at = pl.ds(pl.multiple_of(zc * wide + (2 * h + e) * side, side), side)
            v = tokens[:, at].astype(jnp.float32)
            g = gain[at].astype(jnp.float32).reshape(1, side)
            normed[zc, y, 2 * h + e] = (v * scale[...] * g).astype(jnp.bfloat16)

    def direct(k, way):
        zc, h = half(k)
        slot = normed.at[zc, y, pl.ds(2 * h, 2)]
        return copy(slot, slot, y_send.at[k, way], y_recv.at[k, way], down if way else up)

    def direct_in(k, way):
        zc, h = half(k)
        slot = normed.at[zc, yp if way else ym, pl.ds(2 * h, 2)]
        return copy(slot, slot, y_send.at[k, way], y_recv.at[k, way], up)

    def forward(k, way):
        zc, h = half(k)
        slot = normed.at[zc, yp if way else ym, 2 * h + way]
        return copy(slot, slot, y_send.at[k, 2 + way], y_recv.at[k, 2 + way], down if way else up)

    def forward_in(k, way):
        zc, h = half(k)
        slot = normed.at[zc, y2, 2 * h + way]
        return copy(slot, slot, y_send.at[k, 2 + way], y_recv.at[k, 2 + way], up)

    def w_first(r):
        p = lax.rem(q + r, 8)
        slot = masked.at[z, own_j, xl]
        return copy(slot, slot, w_send.at[r], w_recv.at[r], dev(z, lax.div(p, 2), lax.rem(p, 2), y))

    def w_first_in(r):
        p = lax.rem(q + 8 - r, 8)
        px, pc = lax.div(p, 2), lax.rem(p, 2)
        slot = masked.at[z, lax.div(px, 2) * 2 + pc, lax.rem(px, 2)]
        return copy(slot, slot, w_send.at[r], w_recv.at[r], sibling)

    def w_ring(offset, to, at_receiver):
        slot = masked.at[lax.rem(z + offset, NZ), pl.ds(2 * c, 2)]
        return copy(slot, slot, wz_send.at[at_receiver], wz_recv.at[at_receiver], dev(to, x, c, y))

    def w_ring_in(offset):
        return w_ring(offset, zp, offset)

    def w_share(offset):
        slot = masked.at[lax.rem(z + offset, NZ), pl.ds(2 * c, 2)]
        return copy(slot, slot, wd_send.at[offset], wd_recv.at[offset], sibling)

    def w_share_in(offset):
        slot = masked.at[lax.rem(z + offset, NZ), pl.ds(2 * (1 - c), 2)]
        return copy(slot, slot, wd_send.at[offset], wd_recv.at[offset], sibling)

    def cot_swap():
        src = cot.at[pl.ds(pl.multiple_of((1 - xl) * group, group), group)]
        return copy(src, cot_in, o_send.at[NY], o_recv.at[NY], beside)

    def proj_swap(away):
        at = lax.rem(y + away, NY)
        return copy(p_out.at[at], p_in.at[at], o_send.at[away], o_recv.at[away], beside)

    def core_swap(k):
        return copy(part.at[lax.rem(k, 2), 0], core_in.at[k], c_send.at[k], c_recv.at[k], sibling)

    def x_term(m, d):
        to = dev(z, (xh if d == 2 else 1 - xh) * 2 + (1 - xl if d else xl), c, y)
        return copy(x_out.at[m, d], x_in.at[m, d], x_send.at[m, d], x_recv.at[m, d], to)

    def z_term(m):
        return copy(z_out.at[m], z_in.at[m], z_send.at[m], z_recv.at[m], dev(chunk(m), x, c, y))

    def send(k):
        direct(k, 0).start()
        direct(k, 1).start()

    def relay(k):
        for way in range(2):
            direct_in(k, way).wait_recv()
            forward(k, way).start()

    def products(k):
        zc, h = half(k)
        slot = lax.rem(k, 2)
        forward_in(k, 0).wait_recv()
        forward_in(k, 1).wait_recv()
        for own in range(2):
            n = normed[zc, :, 2 * h + (c if own else 1 - c)].reshape(group, side)
            d = jnp.dot(cot_t[...], n, preferred_element_type=jnp.float32)
            part[slot, own] = d.reshape(2, side, side)
            if not own:
                core_swap(k).start()

    def add_cores(k, far):
        m, slot = lax.div(k, 2), lax.rem(k, 2)
        core_swap(k).wait()
        if far:
            for u in range(2):
                x_out[m, u] = (part[slot, 1, u] + core_in[k, u]).astype(jnp.bfloat16)
                x_term(m, u).start()
        else:
            x_out[m, 2] = (part[slot, 1, 1] + core_in[k, 1]).astype(jnp.bfloat16)
            x_term(m, 2).start()
            keep[lax.rem(m, 2)] = part[slot, 1, 0] + core_in[k, 0]

    def gradient_block(m):
        for d in range(3):
            x_term(m, d).wait_recv()
        terms = [x_in[m, d].astype(jnp.float32) for d in range(3)]
        return keep[lax.rem(m, 2)] + (terms[0] + terms[1] + terms[2])

    def project(m):
        zc = chunk(m)

        @pl.loop(0, 4)
        def _(j):
            n = normed[zc, :, j].reshape(group, side)
            for u in range(2):
                w = masked[zc, j, lax.rem(xl + u, 2)]
                d = jnp.dot(n, w, preferred_element_type=jnp.float32)
                acc[u] += d.reshape(NY, rows, side)

    def project_rows(k, at):
        zc, h = half(k)
        for e in range(2):
            n = normed[zc, at, 2 * h + e]
            for u in range(2):
                w = masked[zc, 2 * h + e, lax.rem(xl + u, 2)]
                acc[u, at] += jnp.dot(n, w, preferred_element_type=jnp.float32)

    normalize(0)
    pl.semaphore_wait(barrier, 16)
    send(0)
    for r in range(1, 8):
        w_first(r).start()
    cot_swap().start()
    for k in range(1, AHEAD):
        normalize(k)
        send(k)

    acc[...] = jnp.zeros_like(acc)
    mine = cot[pl.ds(pl.multiple_of(xl * group, group), group), :]
    cot_t[pl.ds(0, side), :] = mine.T

    @pl.loop(0, NZ)
    def _(m):
        for e in range(2):
            k = 2 * m + e
            relay(k)
            for way in range(2):
                direct(k, way).wait_send()

            @pl.when(k < steps - AHEAD)
            def _():
                normalize(k + AHEAD)
                send(k + AHEAD)

            if e == 0:

                @pl.when(m == 1)
                def _():
                    cot_swap().wait_recv()
                    cot_t[pl.ds(side, side), :] = cot_in[...].T

                @pl.when((m >= 2) & (m <= 5))
                def _():
                    hop = m - 1
                    w_ring_in(8 - hop).wait_recv()
                    w_share(8 - hop).start()

                    @pl.when(hop < 4)
                    def _():
                        w_ring(8 - hop, zp, 7 - hop).start()
                        w_ring_in(hop).wait_recv()
                        w_share(hop).start()

                    @pl.when(hop < 3)
                    def _():
                        w_ring(hop, zm, hop + 1).start()

                @pl.when(m >= 3)
                def _():
                    z_out[m - 3] = gradient_block(m - 3).astype(z_out.dtype)
                    z_term(m - 3).start()

                @pl.when(m >= 2)
                def _():
                    add_cores(k - 3, False)

                @pl.when(m >= 1)
                def _():
                    products(k - 2)

                @pl.when(m == NZ - 1)
                def _():
                    for away in (1, 3):
                        for n in range(-4, 0):
                            project_rows(k + n, lax.rem(y + away, NY))

            else:

                @pl.when(m == 0)
                def _():
                    for r in range(1, 8):
                        w_first_in(r).wait_recv()
                    w_ring(0, zp, 7).start()
                    w_ring(0, zm, 1).start()

                @pl.when(m == NZ - 1)
                def _():
                    for away in (1, 3):
                        at = lax.rem(y + away, NY)
                        for n in range(-1, 1):
                            project_rows(k + n, at)
                        p_out[at] = acc[1, at].astype(jnp.bfloat16)
                        proj_swap(away).start()

                @pl.when((m >= 2) & (m < NZ - 1))
                def _():
                    w_share_in(m - 1).wait_recv()
                    project(m - 2)

                @pl.when(m == NZ - 2)
                def _():
                    w_share_in(NZ - 2).wait_recv()
                    w_share_in(NZ - 1).wait_recv()
                    for n in range(-3, 3):
                        project_rows(k + n, y)
                    p_out[y] = acc[1, y].astype(jnp.bfloat16)
                    proj_swap(0).start()

                @pl.when(m == NZ - 1)
                def _():
                    z_out[NZ - 3] = gradient_block(NZ - 3).astype(z_out.dtype)
                    z_term(NZ - 3).start()

                @pl.when(m >= 1)
                def _():
                    add_cores(k - 3, True)

                @pl.when(m >= 1)
                def _():
                    products(k - 2)

    last = steps - 1
    products(last - 1)
    add_cores(last - 2, False)
    for k in range(last - 5, last):
        project_rows(k, y2)
    add_cores(last - 1, True)
    products(last)
    add_cores(last, False)
    project_rows(last, y2)
    p_out[y2] = acc[1, y2].astype(jnp.bfloat16)
    proj_swap(2).start()
    z_out[NZ - 2] = gradient_block(NZ - 2).astype(z_out.dtype)
    z_term(NZ - 2).start()
    proj[pl.ds(pl.multiple_of(xl * group, group), group), :] = acc[0].reshape(group, side).astype(jnp.bfloat16)

    total = gradient_block(NZ - 1)
    for m in range(NZ - 1):
        z_term(m).wait_recv()
        total = total + z_in[m].astype(jnp.float32)
    total = total.T
    for a in range(side // BLOCK):
        for b in range(side // BLOCK):
            m = mask[a, b].astype(jnp.float32)
            grad[pl.ds(a * BLOCK, BLOCK), pl.ds(b * BLOCK, BLOCK)] = (
                total[a * BLOCK : (a + 1) * BLOCK, b * BLOCK : (b + 1) * BLOCK] * m
            )

    for away in (0, 1, 3, 2):
        proj_swap(away).wait_recv()
    proj[pl.ds(pl.multiple_of((1 - xl) * group, group), group), :] = p_in[...].reshape(group, side)

    @pl.loop(0, steps)
    def _(k):
        forward(k, 0).wait_send()
        forward(k, 1).wait_send()

    @pl.loop(0, NZ)
    def _(m):
        for d in range(3):
            x_term(m, d).wait_send()

    @pl.loop(0, NZ - 1)
    def _(m):
        w_first(m + 1).wait_send()
        w_ring_in(m + 1).wait_send()
        w_share(m + 1).wait_send()
        z_term(m).wait_send()

    cot_swap().wait_send()
    for away in range(NY):
        proj_swap(away).wait_send()


def hand_over(proj_in, grad_in, proj, grad):
    proj[...] = proj_in[...]
    grad[...] = grad_in[...]


def per_device(tokens, gain, kv_weight, block_mask, cotangent):
    rows, width = tokens.shape
    side = kv_weight.shape[0]
    group = NY * rows
    bf16, f32 = jnp.bfloat16, jnp.float32
    dma = pltpu.SemaphoreType.DMA
    vmem = pl.BlockSpec(memory_space=pltpu.VMEM)
    pairs = [(2 * NZ, 4), (8,), (NZ,), (NZ,), (2 * NZ,), (NZ, 3), (NZ,), (NY + 1,)]
    results = pl.pallas_call(
        kernel,
        out_shape=(
            jax.ShapeDtypeStruct(cotangent.shape, bf16),
            jax.ShapeDtypeStruct(kv_weight.shape, f32),
        ),
        in_specs=[pl.BlockSpec(memory_space=pl.ANY), vmem, vmem, pl.BlockSpec(memory_space=pltpu.SMEM), vmem],
        out_specs=(vmem, vmem),
        scratch_shapes=[
            pltpu.VMEM((rows, width), bf16),
            pltpu.VMEM((NZ, NY, 4, rows, side), bf16),
            pltpu.VMEM((rows, side), f32),
            pltpu.VMEM((NZ, 4, 2, side, side), bf16),
            pltpu.VMEM((group, side), bf16),
            pltpu.VMEM((2 * side, group), bf16),
            pltpu.VMEM((2, 2, 2, side, side), f32),
            pltpu.VMEM((2 * NZ, 2, side, side), f32),
            pltpu.VMEM((2, side, side), f32),
            pltpu.VMEM((NZ, 3, side, side), bf16),
            pltpu.VMEM((NZ, 3, side, side), bf16),
            pltpu.VMEM((NZ - 1, side, side), bf16),
            pltpu.VMEM((NZ - 1, side, side), bf16),
            pltpu.VMEM((2, NY, rows, side), f32),
            pltpu.VMEM((NY, rows, side), bf16),
            pltpu.VMEM((NY, rows, side), bf16),
        ]
        + [dma(shape) for shape in pairs for _ in range(2)]
        + [dma((4,))],
        compiler_params=pltpu.CompilerParams(
            collective_id=0, has_side_effects=True, vmem_limit_bytes=60 * 1024 * 1024
        ),
        cost_estimate=pl.CostEstimate(
            flops=8 * group * width * side, bytes_accessed=2 * rows * width, transcendentals=rows
        ),
    )(tokens, gain, kv_weight, block_mask, cotangent)
    return pl.pallas_call(
        hand_over,
        out_shape=tuple(jax.ShapeDtypeStruct(r.shape, r.dtype) for r in results),
        in_specs=[vmem] * 2,
        out_specs=(vmem,) * 2,
    )(*results)


def solution(mesh):
    return jax.shard_map(
        per_device,
        mesh=mesh,
        in_specs=(
            P(("fsdp", "tensor"), None),
            P(),
            P("fsdp", "tensor"),
            P("fsdp", "tensor"),
            P("fsdp", "tensor"),
        ),
        out_specs=(P("fsdp", "tensor"), P("fsdp", "tensor")),
        check_vma=False,
    )
```
